128 devices in a mesh: img: 2 (over core), band: 64 (over z, y, x).
Axes of the slice: x: 4, y: 4, z: 4, core: 2. Of those that a mesh axis runs over, the one named last changes fastest.
Arguments:
- latent: bfloat16 [8, 256, 32, 1280], P('img', 'band'), parts along dimension 0, may hold values from -80 to 80
- stale_act: bfloat16 [8, 256, 32, 1280], P('img', 'band'), parts along dimension 0, may hold values from -4 to 4
- stale_kv: bfloat16 [2, 8, 256, 32, 640], P(None, 'img', 'band'), parts along dimension 1, may hold values from -600 to 600
- timestep: int32 [8, 8], P('img'), parts along dimension 0, may hold values from 0 to 999
- norm_gain: float32 [1280], replicated, may hold values from 0.1 to 1.9
- norm_shift: float32 [1280], replicated, may hold values from -1 to 1
- conv_weight: bfloat16 [3, 3, 1280, 640], replicated, may hold values from -0.0546875 to 0.0546875
- time_weight: bfloat16 [1280, 640], replicated, may hold values from -0.15625 to 0.15625
- attn_in: bfloat16 [1280, 1920], replicated, may hold values from -0.15625 to 0.15625
- attn_out: bfloat16 [640, 1280], replicated, may hold values from -0.25 to 0.25
Outputs:
- block_out: bfloat16 [8, 256, 32, 1280], P('img', 'band'), parts along dimension 0
- fresh_kv: bfloat16 [2, 8, 256, 32, 640], P(None, 'img', 'band'), parts along dimension 1
The draws below stay inside these ranges and needn't reach their ends.
There are 2 independent parts, one for each index of `img`. The reference program is written for one: setup_inputs(seed, part) draws one part's arguments, and reference() takes and returns one part's arrays. A program takes and returns all parts, laid end to end along the dimension named above; an argument that names none is the same for every part. Nothing has to cross between parts.
All inputs are finite; a program needn't handle non-finite values.
Results may differ from the reference program's by a relative error of at most 0.0055.
Values may be sent and summed in bfloat16 or wider, within the bound.
No kernel may reach another device: no remote copies, remote signals or barrier semaphores. Data moves between devices by JAX's collectives and lax.ppermute only.
A program may use at most 192 MiB of HBM per device.

```python
import math
import jax
import jax.numpy as jnp
from jax import lax

IMAGES = 4
ROWS_DEV = 4
IMG_ROWS = 32
COLS = 32
CH = 1280
GROUPS = 32
CONV_OUT = 640
HEADS = 10
HEAD_DIM = 64
TDIM = 1280
INNER = 640
ROWS = 256


def draw_latent(key, part):
    subkeys = jax.random.split(key, 3)
    shape = (IMAGES, ROWS, COLS, CH)
    base = jax.random.truncated_normal(subkeys[0], -4.0, 4.0, shape, jnp.float32)
    row_index = jnp.arange(ROWS)
    image_row = row_index // ROWS_DEV // (ROWS // IMG_ROWS) * ROWS_DEV + row_index % ROWS_DEV
    rising = 1.0 + 2.0 * image_row.astype(jnp.float32) / (IMG_ROWS - 1)
    row_factor = jnp.exp(jax.random.uniform(subkeys[1], (IMAGES, ROWS, 1, 1), jnp.float32, -0.35, 0.35))
    channel_factor = jnp.exp(jax.random.uniform(subkeys[2], (CH,), jnp.float32, math.log(0.4), math.log(4.0)))
    return (base * rising[None, :, None, None] * row_factor * channel_factor).astype(jnp.bfloat16)


def draw_stale_kv(key, part):
    subkeys = jax.random.split(key, 1)
    shape = (2, IMAGES, ROWS, COLS, HEADS * HEAD_DIM)
    base = jax.random.truncated_normal(subkeys[0], -4.0, 4.0, shape, jnp.float32)
    scaled = base * jnp.array([1.5, 2.5], jnp.float32)[:, None, None, None, None]
    return scaled.astype(jnp.bfloat16)


def touch_ends(entries, key, low, high):
    extent = entries.shape
    spot = [jax.random.randint(jax.random.fold_in(key, axis), (), 0, extent[axis]) for axis in range(len(extent))]
    entries = entries.at[tuple(spot)].set(low)
    longest = extent.index(max(extent))
    spot[longest] = (spot[longest] + 1) % extent[longest]
    return entries.at[tuple(spot)].set(high)


def block_scale(own_key, extent, cuts, smallest, high):
    loudness, own = 1.0, jax.random.fold_in(own_key, 6)
    for dim, parts in cuts:
        heights = jnp.exp(jax.random.uniform(jax.random.fold_in(own, dim), (parts,), jnp.float32, smallest / len(cuts), high / len(cuts)))
        loudness = loudness * jnp.repeat(heights, extent[dim] // parts).reshape([-1 if axis == dim else 1 for axis in range(len(extent))])
    return loudness


def gaussian(key, extent, scale, limit, shards=(), kind=jnp.bfloat16):
    factor_of = block_scale(key, extent, shards, -0.22, 0.18) if shards else 1.0
    values = jax.random.normal(key, extent, jnp.float32) * scale * factor_of
    return jnp.minimum(jnp.maximum(values, -limit), limit).astype(kind)


def setup_inputs(seed: int = 0, part: int = 0) -> dict:
    key_of = jax.random.split(jax.random.key(seed), 11)
    part_splits = jax.random.split(jax.random.fold_in(key_of[10], part), 11)
    latent = draw_latent(jax.random.fold_in(jax.random.fold_in(key_of[10], part), 71), part)
    stale_act = gaussian(part_splits[1], (IMAGES, ROWS, COLS, CH), 0.7, 4.0, ((1, 64),))
    stale_kv = draw_stale_kv(jax.random.fold_in(jax.random.fold_in(key_of[10], part), 71), part)
    timestep = touch_ends(jax.random.randint(part_splits[3], (IMAGES, ROWS // IMG_ROWS), 0, 1000), jax.random.fold_in(part_splits[3], 1), 0, 999).astype(jnp.int32)
    norm_gain = jnp.clip(1.0 + 0.18 * jax.random.normal(key_of[4], (CH,), jnp.float32), 0.1, 1.9)
    norm_shift = jnp.clip(jax.random.uniform(key_of[5], (CH,), jnp.float32, -1.0, 1.0), -1.0, 1.0)
    conv_weight = gaussian(key_of[6], (3, 3, CH, CONV_OUT), (9 * CH) ** -0.5, 0.0546875)
    time_weight = gaussian(key_of[7], (TDIM, CONV_OUT), TDIM ** -0.5, 0.15625)
    attn_in = gaussian(key_of[8], (CH, 3 * INNER), CH ** -0.5, 0.15625)
    attn_out = gaussian(key_of[9], (INNER, CH), INNER ** -0.5, 0.25)
    return dict(latent=latent, stale_act=stale_act, stale_kv=stale_kv, timestep=timestep, norm_gain=norm_gain, norm_shift=norm_shift, conv_weight=conv_weight, time_weight=time_weight, attn_in=attn_in, attn_out=attn_out)


def time_term(timestep, time_weight):
    half_dim = TDIM // 2
    frequency = jnp.exp(-math.log(10000.0) * jnp.arange(half_dim, dtype=jnp.float32) / half_dim)
    angles = timestep.astype(jnp.float32)[:, None] * frequency[None, :]
    embedding = jnp.concatenate([jnp.cos(angles), jnp.sin(angles)], axis=1)
    return jnp.dot(jax.nn.silu(embedding), time_weight.astype(jnp.float32), precision=lax.Precision.HIGHEST)

def to_images(array, axis):
    shape = array.shape
    split = shape[:axis] + (IMG_ROWS // ROWS_DEV, ROWS // IMG_ROWS, ROWS_DEV) + shape[axis + 1:]
    return jnp.swapaxes(array.reshape(split), axis, axis + 1).reshape(shape)

def to_bands(array, axis):
    shape = array.shape
    split = shape[:axis] + (ROWS // IMG_ROWS, IMG_ROWS // ROWS_DEV, ROWS_DEV) + shape[axis + 1:]
    return jnp.swapaxes(array.reshape(split), axis, axis + 1).reshape(shape)

def reference(latent, stale_act, stale_kv, timestep, norm_gain, norm_shift, conv_weight, time_weight, attn_in, attn_out):
    stacked = ROWS // IMG_ROWS
    latent = to_images(latent, 1)
    stale_act = to_images(stale_act, 1)
    stale_kv = to_images(stale_kv, 2)
    floats = latent.astype(jnp.float32)
    per_group = CH // GROUPS
    grouped = floats.reshape(IMAGES, stacked, IMG_ROWS * COLS, GROUPS, per_group)
    center = lax.optimization_barrier(jnp.mean(grouped, axis=(2, 4), keepdims=True))
    spread = lax.optimization_barrier(jnp.mean((grouped - center) ** 2, axis=(2, 4), keepdims=True))
    normed = ((grouped - center) / jnp.sqrt(spread + 1e-05)).reshape(IMAGES, ROWS, COLS, CH)
    activated = jax.nn.silu(normed * norm_gain + norm_shift).astype(jnp.bfloat16)
    position = jnp.arange(ROWS) % ROWS_DEV
    in_image = jnp.arange(ROWS) % IMG_ROWS
    blank = jnp.zeros((IMAGES, 1, COLS, CH), jnp.bfloat16)
    zeros_full = jnp.zeros((IMAGES, ROWS, COLS, CH), jnp.bfloat16)
    above = jnp.where((position == 0)[None, :, None, None], jnp.concatenate([blank, stale_act[:, :-1]], axis=1), jnp.concatenate([blank, activated[:, :-1]], axis=1))
    above = jnp.where((in_image == 0)[None, :, None, None], zeros_full, above)
    below = jnp.where((position == ROWS_DEV - 1)[None, :, None, None], jnp.concatenate([stale_act[:, 1:], blank], axis=1), jnp.concatenate([activated[:, 1:], blank], axis=1))
    below = jnp.where((in_image == IMG_ROWS - 1)[None, :, None, None], zeros_full, below)
    kernel = conv_weight.astype(jnp.float32)
    convolved = jnp.zeros((IMAGES, ROWS, COLS, CONV_OUT), jnp.float32)
    for row_tap, source in enumerate((above, activated, below)):
        padded = jnp.pad(source.astype(jnp.float32), ((0, 0), (0, 0), (1, 1), (0, 0)))
        for col_tap in range(3):
            convolved = convolved + jnp.einsum('bhwc,cd->bhwd', padded[:, :, col_tap:col_tap + COLS], kernel[row_tap, col_tap], precision=lax.Precision.HIGHEST)
    time_bias = time_term(timestep.reshape(-1), time_weight).reshape(IMAGES, stacked, CONV_OUT)
    time_rows = jnp.repeat(time_bias, IMG_ROWS, axis=1)
    window = (floats[..., :CONV_OUT] + convolved + time_rows[:, :, None, :]).astype(jnp.bfloat16)
    hidden = jnp.concatenate([window, latent[..., CONV_OUT:]], axis=-1)
    widened = hidden.astype(jnp.float32)
    token_mean = lax.optimization_barrier(jnp.mean(widened, axis=-1, keepdims=True))
    token_var = lax.optimization_barrier(jnp.mean((widened - token_mean) ** 2, axis=-1, keepdims=True))
    normalized = ((widened - token_mean) / jnp.sqrt(token_var + 1e-05)).astype(jnp.bfloat16)
    projected = jnp.dot(normalized.reshape(-1, CH), attn_in, preferred_element_type=jnp.float32)
    projected = projected.astype(jnp.bfloat16).reshape(IMAGES, ROWS, COLS, 3 * INNER)
    queries = projected[..., :INNER]
    fresh_kv = jnp.stack([projected[..., INNER:2 * INNER], projected[..., 2 * INNER:]])
    batch_all = IMAGES * stacked
    fresh_six = fresh_kv.reshape(2, batch_all, IMG_ROWS, COLS, INNER)
    stale_six = stale_kv.reshape(2, batch_all, IMG_ROWS, COLS, INNER)
    query_all = queries.reshape(batch_all, IMG_ROWS, COLS, INNER)
    results = []
    for band_place in range(IMG_ROWS // ROWS_DEV):
        owned = (jnp.arange(IMG_ROWS) // ROWS_DEV == band_place)[None, None, :, None, None]
        mixed = jnp.where(owned, fresh_six, stale_six).astype(jnp.float32)
        key_heads = mixed[0].reshape(batch_all, IMG_ROWS * COLS, HEADS, HEAD_DIM)
        value_heads = mixed[1].reshape(batch_all, IMG_ROWS * COLS, HEADS, HEAD_DIM)
        query_heads = query_all[:, band_place * ROWS_DEV:(band_place + 1) * ROWS_DEV].astype(jnp.float32)
        query_heads = query_heads.reshape(batch_all, ROWS_DEV * COLS, HEADS, HEAD_DIM)
        scores = jnp.einsum('bqhd,bkhd->bhqk', query_heads, key_heads, precision=lax.Precision.HIGHEST) * HEAD_DIM ** (-0.5)
        peak = lax.optimization_barrier(jnp.max(scores, axis=-1, keepdims=True))
        exponent = jnp.exp(scores - peak)
        total = lax.optimization_barrier(jnp.sum(exponent, axis=-1))
        weights = lax.optimization_barrier(exponent.astype(jnp.bfloat16)).astype(jnp.float32)
        context = jnp.einsum('bhqk,bkhd->bqhd', weights, value_heads, precision=lax.Precision.HIGHEST)
        context = context / jnp.transpose(total, (0, 2, 1))[..., None]
        results.append(context.astype(jnp.bfloat16).reshape(batch_all, ROWS_DEV, COLS, INNER))
    attended = jnp.concatenate(results, axis=1).reshape(IMAGES, ROWS, COLS, INNER)
    update = jnp.dot(attended.reshape(-1, INNER), attn_out, preferred_element_type=jnp.float32)
    block_out = (widened + update.reshape(IMAGES, ROWS, COLS, CH)).astype(jnp.bfloat16)
    return (to_bands(block_out, 1), to_bands(fresh_kv, 2))
```

```python
import math

import jax
import jax.numpy as jnp
from jax import lax
from jax.experimental import pallas as pl
from jax.experimental.pallas import tpu as pltpu
from jax.sharding import PartitionSpec as P

IMG_ROWS = 32
GROUPS = 32
HEADS = 10
TDIM = 1280
LANES = 128
MIB = 1 << 20
STACK = 8


def rotated(value, by):
    count = lax.axis_size("band")
    return lax.ppermute(value, "band", [(i, (i + by) % count) for i in range(count)])


def shifted(value, by):
    count = lax.axis_size("band")
    pairs = [(i, i + by) for i in range(count) if 0 <= i + by < count]
    return lax.ppermute(value, "band", pairs)


def flipped(value, bit):
    count = lax.axis_size("band")
    return lax.ppermute(value, "band", [(i, i ^ (bit * STACK)) for i in range(count)])


def time_term(timestep, time_weight):
    half_dim = TDIM // 2
    frequency = jnp.exp(-math.log(10000.0) * jnp.arange(half_dim, dtype=jnp.float32) / half_dim)
    angles = timestep.astype(jnp.float32)[:, None] * frequency[None, :]
    embedding = jnp.concatenate([jnp.cos(angles), jnp.sin(angles)], axis=1)
    return jnp.dot(
        jax.nn.silu(embedding), time_weight.astype(jnp.float32), precision=lax.Precision.HIGHEST
    )


def group_matrix(channels, per_group, transposed):
    shape = (LANES, channels) if transposed else (channels, LANES)
    channel = lax.broadcasted_iota(jnp.int32, shape, 1 if transposed else 0)
    first = lax.broadcasted_iota(jnp.int32, shape, 0 if transposed else 1) * per_group
    return jnp.where((channel >= first) & (channel < first + per_group), 1.0, 0.0)


def exact_dot(left, right):
    return jnp.dot(
        left, right, precision=lax.Precision.HIGHEST, preferred_element_type=jnp.float32
    )


def stats_kernel(latent, out, sums):
    images, tokens, channels = latent.shape
    per_group = channels // GROUPS
    gather = group_matrix(channels, per_group, False)
    spread = group_matrix(channels, per_group, True)
    sums[...] = jnp.zeros_like(sums)
    for i in range(images):
        sums[i : i + 1, :] = jnp.sum(latent[i].astype(jnp.float32), axis=0, keepdims=True)
    mean = exact_dot(sums[...], gather) * (1.0 / (tokens * per_group))
    center = exact_dot(mean, spread)
    for i in range(images):
        deviation = latent[i].astype(jnp.float32) - center[i : i + 1, :]
        sums[i : i + 1, :] = jnp.sum(deviation * deviation, axis=0, keepdims=True)
    out[0] = mean
    out[1] = exact_dot(sums[...], gather)


def local_stats(latent):
    images, tokens, channels = latent.shape
    return pl.pallas_call(
        stats_kernel,
        out_shape=jax.ShapeDtypeStruct((2, 8, LANES), jnp.float32),
        scratch_shapes=[pltpu.VMEM((8, channels), jnp.float32)],
        compiler_params=pltpu.CompilerParams(vmem_limit_bytes=24 * MIB),
        cost_estimate=pl.CostEstimate(
            flops=8 * latent.size, bytes_accessed=2 * latent.size, transcendentals=0
        ),
        name="group_stats",
    )(latent)


def merged(own, other, count):
    gap = own[0] - other[0]
    return jnp.stack([(own[0] + other[0]) * 0.5, own[1] + other[1] + gap * gap * (count * 0.5)])


def conv_kernel(
    counted,
    stats,
    gain,
    shift,
    bias,
    latent,
    top,
    bottom,
    conv_hbm,
    attn_hbm,
    hidden,
    normal,
    queries,
    ext,
    weights,
    query_weight,
    acc,
    scales,
    sems,
):
    images, tokens, channels = latent.shape
    columns = top.shape[1]
    height = tokens // columns
    width = acc.shape[1]
    slab = images * columns
    inner = query_weight.shape[1]
    copies = [
        pltpu.make_async_copy(conv_hbm.at[dy], weights.at[dy], sems.at[dy]) for dy in range(3)
    ]
    copies.append(pltpu.make_async_copy(attn_hbm.at[:, :inner], query_weight, sems.at[3]))
    for copy in copies:
        copy.start()
    spread = group_matrix(channels, channels // GROUPS, True)
    scales[0] = exact_dot(stats[0], spread)
    inverse = 1.0 / jnp.sqrt(stats[1] * (1.0 / counted) + 1e-05)
    scales[1] = exact_dot(inverse, spread) * gain[...]
    place = lax.broadcasted_iota(jnp.int32, (columns, channels), 0)

    def put(value, row, i):
        rows = pl.ds(pl.multiple_of(row * slab + i * columns, columns), columns)
        before = jnp.where(place == 0, 0.0, pltpu.roll(value, 1, 0))
        after = jnp.where(place == columns - 1, 0.0, pltpu.roll(value, columns - 1, 0))
        ext[rows, 0:channels] = before.astype(jnp.bfloat16)
        ext[rows, channels : 2 * channels] = value.astype(jnp.bfloat16)
        ext[rows, 2 * channels : 3 * channels] = after.astype(jnp.bfloat16)

    def fill(i, carry):
        center = scales[0, pl.ds(i, 1), :]
        factor = scales[1, pl.ds(i, 1), :]
        put(top[i].astype(jnp.float32), 0, i)
        put(bottom[i].astype(jnp.float32), height + 1, i)
        for y in range(height):
            value = latent[i, y * columns : (y + 1) * columns, :].astype(jnp.float32)
            value = (value - center) * factor + shift[...]
            put(value / (1.0 + jnp.exp(-value)), y + 1, i)
        return carry

    lax.fori_loop(0, images, fill, 0)
    for dy in range(3):
        copies[dy].wait()
        part = jnp.dot(
            ext[dy * slab : (dy + height) * slab, :],
            weights[dy],
            preferred_element_type=jnp.float32,
        )
        if dy == 0:
            acc[...] = part
        else:
            acc[...] += part

    def finish(i, carry):
        for y in range(height):
            tokens_of = slice(y * columns, (y + 1) * columns)
            rows = pl.ds(pl.multiple_of(y * slab + i * columns, columns), columns)
            window = latent[i, tokens_of, :width].astype(jnp.float32) + acc[rows, :]
            window = (window + bias[pl.ds(i, 1), :]).astype(jnp.bfloat16)
            whole = jnp.concatenate([window, latent[i, tokens_of, width:]], axis=-1)
            hidden[i, tokens_of, :] = whole
            wide = whole.astype(jnp.float32)
            wide = wide - jnp.mean(wide, axis=-1, keepdims=True)
            variance = jnp.mean(wide * wide, axis=-1, keepdims=True)
            normal[i, tokens_of, :] = (wide * (1.0 / jnp.sqrt(variance + 1e-05))).astype(
                jnp.bfloat16
            )
        return carry

    lax.fori_loop(0, images, finish, 0)
    copies[3].wait()
    found = jnp.dot(
        normal[...].reshape(images * tokens, channels),
        query_weight[...],
        preferred_element_type=jnp.float32,
    )
    found = found.astype(jnp.bfloat16) * jnp.bfloat16((inner // HEADS) ** -0.5)
    queries[...] = found.reshape(images, tokens, inner)


def convolve(stats, gain, shift, bias, latent, top, bottom, conv_weight, attn_in, counted):
    images, tokens, channels = latent.shape
    columns = top.shape[1]
    width = conv_weight.shape[-1]
    inner = attn_in.shape[1] // 3
    slab = images * columns
    vmem = pl.BlockSpec(memory_space=pltpu.VMEM)
    anywhere = pl.BlockSpec(memory_space=pl.ANY)

    def body(*refs):
        conv_kernel(counted, *refs)

    return pl.pallas_call(
        body,
        out_shape=(
            jax.ShapeDtypeStruct(latent.shape, jnp.bfloat16),
            jax.ShapeDtypeStruct(latent.shape, jnp.bfloat16),
            jax.ShapeDtypeStruct((images, tokens, inner), jnp.bfloat16),
        ),
        in_specs=[vmem] * 7 + [anywhere] * 2,
        out_specs=(vmem,) * 3,
        scratch_shapes=[
            pltpu.VMEM(((tokens // columns + 2) * slab, 3 * channels), jnp.bfloat16),
            pltpu.VMEM((3, 3 * channels, width), jnp.bfloat16),
            pltpu.VMEM((channels, inner), jnp.bfloat16),
            pltpu.VMEM((images * tokens, width), jnp.float32),
            pltpu.VMEM((2, 8, channels), jnp.float32),
            pltpu.SemaphoreType.DMA((4,)),
        ],
        compiler_params=pltpu.CompilerParams(vmem_limit_bytes=48 * MIB),
        cost_estimate=pl.CostEstimate(
            flops=2 * images * tokens * channels * (9 * width + inner),
            bytes_accessed=2 * (conv_weight.size + channels * inner + 5 * latent.size),
            transcendentals=latent.size,
        ),
        name="conv_queries",
    )(stats, gain, shift, bias, latent, top, bottom, conv_weight, attn_in)


def project_kernel(normal, weight, out):
    images, tokens, channels = normal.shape
    found = jnp.dot(
        normal[...].reshape(images * tokens, channels),
        weight[...],
        preferred_element_type=jnp.float32,
    )
    out[0] = found.astype(jnp.bfloat16).reshape(out.shape[1:])


def project(normal, attn_in):
    images, tokens, channels = normal.shape
    inner = attn_in.shape[1] // 3
    return pl.pallas_call(
        project_kernel,
        grid=(2,),
        out_shape=jax.ShapeDtypeStruct((2, images, tokens, inner), jnp.bfloat16),
        in_specs=[
            pl.BlockSpec(normal.shape, lambda j: (0, 0, 0)),
            pl.BlockSpec((channels, inner), lambda j: (0, j + 1)),
        ],
        out_specs=pl.BlockSpec((1, images, tokens, inner), lambda j: (j, 0, 0, 0)),
        compiler_params=pltpu.CompilerParams(vmem_limit_bytes=24 * MIB),
        cost_estimate=pl.CostEstimate(
            flops=4 * images * tokens * channels * inner,
            bytes_accessed=4 * (channels * inner + normal.size),
            transcendentals=0,
        ),
        name="keys_values",
    )(normal, attn_in)


def attend_kernel(queries, first, second, third, fourth, out, logs):
    tokens, inner = queries.shape[1:]
    size = inner // HEADS
    pair = 2 * size
    lane = lax.broadcasted_iota(jnp.int32, (tokens, pair), 1)
    low = lane < size
    sources = (first, second, third, fourth)
    found = jnp.zeros((tokens, LANES), jnp.float32)
    spot = lax.broadcasted_iota(jnp.int32, (tokens, LANES), 1)
    for p in range(HEADS // 2):
        lanes = slice(p * pair, (p + 1) * pair)
        query = queries[0, :, lanes]
        blank = jnp.zeros_like(query)
        both = jnp.concatenate(
            [jnp.where(low, query, blank), jnp.where(low, blank, query)], axis=0
        )
        keys = jnp.concatenate([s[0, 0, :, lanes] for s in sources], axis=0)
        values = jnp.concatenate([s[1, 0, :, lanes] for s in sources], axis=0)
        scores = lax.dot_general(
            both, keys, (((1,), (1,)), ((), ())), preferred_element_type=jnp.float32
        )
        peak = jnp.max(scores, axis=-1, keepdims=True)
        exponent = jnp.exp(scores - peak)
        total = jnp.sum(exponent, axis=-1, keepdims=True)
        context = jnp.dot(
            exponent.astype(jnp.bfloat16), values, preferred_element_type=jnp.float32
        )
        context = context * (1.0 / total)
        out[0, :, lanes] = jnp.where(low, context[:tokens], context[tokens:]).astype(out.dtype)
        level = peak + jnp.log(total)
        found = jnp.where(spot == 2 * p, level[:tokens], found)
        found = jnp.where(spot == 2 * p + 1, level[tokens:], found)
    logs[0] = jnp.transpose(found)[: logs.shape[1], :]


def attend(queries, first, second, third, fourth, start, images, dtype):
    tokens, inner = queries.shape[1:]
    kv_spec = pl.BlockSpec((2, 1, tokens, inner), lambda i: (0, i + start, 0, 0))
    elements = images * HEADS * tokens * 4 * tokens
    return pl.pallas_call(
        attend_kernel,
        grid=(images,),
        out_shape=(
            jax.ShapeDtypeStruct((images, tokens, inner), dtype),
            jax.ShapeDtypeStruct((images, 16, tokens), jnp.float32),
        ),
        in_specs=[pl.BlockSpec((1, tokens, inner), lambda i: (i, 0, 0))] + [kv_spec] * 4,
        out_specs=(
            pl.BlockSpec((1, tokens, inner), lambda i: (i, 0, 0)),
            pl.BlockSpec((1, 16, tokens), lambda i: (i, 0, 0)),
        ),
        compiler_params=pltpu.CompilerParams(vmem_limit_bytes=24 * MIB),
        cost_estimate=pl.CostEstimate(
            flops=4 * elements * 256,
            bytes_accessed=images * tokens * inner * 24,
            transcendentals=elements,
        ),
        name="attend",
    )(queries, first, second, third, fourth)


def join_kernel(own, own_logs, far, far_logs, hidden, weight, out, attended):
    images, tokens, inner = own.shape
    size = inner // HEADS
    pair = 2 * size
    low = lax.broadcasted_iota(jnp.int32, (tokens, pair), 1) < size
    for i in range(images):
        here, there = own_logs[i], far_logs[i]
        top = jnp.maximum(here, there)
        here, there = jnp.exp(here - top), jnp.exp(there - top)
        share = there * (1.0 / (here + there))
        share = jnp.concatenate(
            [share, jnp.zeros((LANES - share.shape[0], tokens), jnp.float32)], axis=0
        )
        share = jnp.transpose(share)
        for p in range(HEADS // 2):
            lanes = slice(p * pair, (p + 1) * pair)
            part = jnp.where(
                low,
                jnp.broadcast_to(share[:, 2 * p : 2 * p + 1], (tokens, pair)),
                jnp.broadcast_to(share[:, 2 * p + 1 : 2 * p + 2], (tokens, pair)),
            )
            mine = own[i, :, lanes].astype(jnp.float32)
            theirs = far[i, :, lanes].astype(jnp.float32)
            attended[i * tokens : (i + 1) * tokens, lanes] = (
                mine * (1.0 - part) + theirs * part
            ).astype(jnp.bfloat16)
    update = jnp.dot(attended[...], weight[...], preferred_element_type=jnp.float32)
    update = update.reshape(out.shape)
    out[...] = (hidden[...].astype(jnp.float32) + update).astype(jnp.bfloat16)


def join(own, own_logs, far, far_logs, hidden, attn_out):
    images, tokens, inner = own.shape
    channels = hidden.shape[-1]
    step = 2

    def spec(rows, lanes):
        return pl.BlockSpec((step, rows, lanes), lambda i: (i, 0, 0))

    return pl.pallas_call(
        join_kernel,
        grid=(images // step,),
        out_shape=jax.ShapeDtypeStruct(hidden.shape, jnp.bfloat16),
        in_specs=[
            spec(tokens, inner),
            spec(16, tokens),
            spec(tokens, inner),
            spec(16, tokens),
            spec(tokens, channels),
            pl.BlockSpec(attn_out.shape, lambda i: (0, 0)),
        ],
        out_specs=spec(tokens, channels),
        scratch_shapes=[pltpu.VMEM((step * tokens, inner), jnp.bfloat16)],
        compiler_params=pltpu.CompilerParams(vmem_limit_bytes=24 * MIB),
        cost_estimate=pl.CostEstimate(
            flops=2 * images * tokens * inner * channels,
            bytes_accessed=2 * attn_out.size + 4 * hidden.size + 6 * own.size,
            transcendentals=0,
        ),
        name="join_project",
    )(own, own_logs, far, far_logs, hidden, attn_out)


def on_device(
    latent,
    stale_act,
    stale_kv,
    timestep,
    norm_gain,
    norm_shift,
    conv_weight,
    time_weight,
    attn_in,
    attn_out,
):
    images, height, columns, channels = latent.shape
    width = conv_weight.shape[3]
    inner = attn_out.shape[0]
    tokens = height * columns
    per_group = channels // GROUPS
    out_shape = latent.shape
    kv_shape = stale_kv.shape
    slot = lax.axis_index("band") % STACK
    latent = latent.reshape(images, tokens, channels)
    stale_kv = stale_kv.reshape(2, images, tokens, inner)

    top = shifted(stale_act[:, height - 1], STACK)
    bottom = shifted(stale_act[:, 0], -STACK)
    kv_up = rotated(stale_kv, 2 * STACK)
    kv_down = rotated(stale_kv, -2 * STACK)
    kv_far = rotated(stale_kv, 4 * STACK)

    stats = local_stats(latent)
    count = tokens * per_group
    for bit in (1, 2, 4):
        stats = merged(stats, flipped(stats, bit), count)
        count *= 2

    own_steps = lax.dynamic_index_in_dim(timestep, slot, 1, keepdims=False)
    bias = time_term(own_steps, time_weight)
    hidden, normal, queries = convolve(
        stats,
        norm_gain.reshape(1, channels),
        norm_shift.reshape(1, channels),
        bias,
        latent,
        top,
        bottom,
        conv_weight.reshape(3, 3 * channels, width),
        attn_in,
        float(count),
    )
    half = images // 2
    far_queries = [flipped(queries[k * half : (k + 1) * half], 1) for k in range(2)]
    fresh_kv = project(normal, attn_in)
    own, own_logs = attend(
        queries, fresh_kv, kv_up, kv_down, kv_far, 0, images, jnp.float32
    )
    far, far_logs = [], []
    for k in range(2):
        context, logs = attend(
            far_queries[k], stale_kv, kv_up, kv_down, kv_far, k * half, half, jnp.bfloat16
        )
        far.append(flipped(context, 1))
        far_logs.append(flipped(logs, 1))
    block_out = join(
        own,
        own_logs,
        jnp.concatenate(far, axis=0),
        jnp.concatenate(far_logs, axis=0),
        hidden,
        attn_out,
    )
    return (block_out.reshape(out_shape), fresh_kv.reshape(kv_shape))


def solution(mesh):
    return jax.shard_map(
        on_device,
        mesh=mesh,
        in_specs=(
            P("img", "band", None, None),
            P("img", "band", None, None),
            P(None, "img", "band", None, None),
            P("img", None),
            P(),
            P(),
            P(),
            P(),
            P(),
            P(),
        ),
        out_specs=(P("img", "band", None, None), P(None, "img", "band", None, None)),
        check_vma=False,
    )
```

```python
import math

import jax
import jax.numpy as jnp
from jax import lax
from jax.experimental import pallas as pl
from jax.experimental.pallas import tpu as pltpu
from jax.sharding import PartitionSpec as P

IMG_ROWS = 32
GROUPS = 32
HEADS = 10
TDIM = 1280
LANES = 128
SLOTS = 16
MIB = 1 << 20
STACK = 8


def rotated(value, by):
    count = lax.axis_size("band")
    return lax.ppermute(value, "band", [(i, (i + by) % count) for i in range(count)])


def flipped(value, bit):
    count = lax.axis_size("band")
    return lax.ppermute(value, "band", [(i, i ^ (bit * STACK)) for i in range(count)])


def time_term(timestep, time_weight):
    half_dim = TDIM // 2
    frequency = jnp.exp(-math.log(10000.0) * jnp.arange(half_dim, dtype=jnp.float32) / half_dim)
    angles = timestep.astype(jnp.float32)[:, None] * frequency[None, :]
    embedding = jnp.concatenate([jnp.cos(angles), jnp.sin(angles)], axis=1)
    return jnp.dot(
        jax.nn.silu(embedding), time_weight.astype(jnp.float32), precision=lax.Precision.HIGHEST
    )


def group_matrix(channels, per_group, transposed):
    shape = (LANES, channels) if transposed else (channels, LANES)
    channel = lax.broadcasted_iota(jnp.int32, shape, 1 if transposed else 0)
    first = lax.broadcasted_iota(jnp.int32, shape, 0 if transposed else 1) * per_group
    return jnp.where((channel >= first) & (channel < first + per_group), 1.0, 0.0)


def exact_dot(left, right):
    return jnp.dot(
        left, right, precision=lax.Precision.HIGHEST, preferred_element_type=jnp.float32
    )


def stats_kernel(latent_hbm, act_hbm, out, last_rows, first_rows, latent, rims, sums, sems):
    images, tokens, channels = latent.shape
    columns = last_rows.shape[1]
    per_group = channels // GROUPS
    copies = [
        pltpu.make_async_copy(latent_hbm.at[i], latent.at[i], sems.at[i]) for i in range(images)
    ]
    for copy in copies:
        copy.start()
    sides = (slice(tokens - columns, tokens), slice(0, columns))
    cuts = [
        pltpu.make_async_copy(act_hbm.at[:, side, :], rims.at[k], sems.at[images + k])
        for k, side in enumerate(sides)
    ]
    for cut in cuts:
        cut.start()
    passed = [
        pltpu.make_async_copy(rims.at[k], rows, sems.at[images + 2 + k])
        for k, rows in enumerate((last_rows, first_rows))
    ]
    gather = group_matrix(channels, per_group, False)
    spread = group_matrix(channels, per_group, True)
    sums[...] = jnp.zeros_like(sums)
    for i in range(images):
        copies[i].wait()
        sums[i : i + 1, :] = jnp.sum(latent[i].astype(jnp.float32), axis=0, keepdims=True)
    for cut, onward in zip(cuts, passed):
        cut.wait()
        onward.start()
    mean = exact_dot(sums[...], gather) * (1.0 / (tokens * per_group))
    center = exact_dot(mean, spread)
    for i in range(images):
        deviation = latent[i].astype(jnp.float32) - center[i : i + 1, :]
        sums[i : i + 1, :] = jnp.sum(deviation * deviation, axis=0, keepdims=True)
    out[0] = mean
    out[1] = exact_dot(sums[...], gather)
    for onward in passed:
        onward.wait()


def local_stats(latent, stale_act, columns):
    images, tokens, channels = latent.shape
    anywhere = pl.BlockSpec(memory_space=pltpu.HBM)
    vmem = pl.BlockSpec(memory_space=pltpu.VMEM)
    rim = jax.ShapeDtypeStruct((images, columns, channels), jnp.bfloat16)
    return pl.pallas_call(
        stats_kernel,
        out_shape=(jax.ShapeDtypeStruct((2, 8, LANES), jnp.float32), rim, rim),
        in_specs=[anywhere] * 2,
        out_specs=(vmem, anywhere, anywhere),
        scratch_shapes=[
            pltpu.VMEM(latent.shape, jnp.bfloat16),
            pltpu.VMEM((2,) + rim.shape, jnp.bfloat16),
            pltpu.VMEM((8, channels), jnp.float32),
            pltpu.SemaphoreType.DMA((images + 4,)),
        ],
        compiler_params=pltpu.CompilerParams(vmem_limit_bytes=60 * MIB),
        cost_estimate=pl.CostEstimate(
            flops=8 * latent.size, bytes_accessed=3 * latent.size, transcendentals=0
        ),
        name="group_stats",
    )(latent, stale_act)


def merged(own, other, count):
    gap = own[0] - other[0]
    return jnp.stack([(own[0] + other[0]) * 0.5, own[1] + other[1] + gap * gap * (count * 0.5)])


def conv_kernel(
    counted,
    inside,
    stats,
    gain,
    shift,
    bias,
    top,
    bottom,
    latent_hbm,
    conv_hbm,
    attn_hbm,
    hidden,
    normal,
    queries,
    latent,
    ext,
    weights,
    query_weight,
    acc,
    scales,
    sems,
):
    images, tokens, channels = latent.shape
    columns = top.shape[1]
    height = tokens // columns
    width = acc.shape[1]
    slab = images * columns
    inner = query_weight.shape[1]
    copies = [
        pltpu.make_async_copy(conv_hbm.at[dy], weights.at[dy], sems.at[dy]) for dy in range(3)
    ]
    copies.append(pltpu.make_async_copy(attn_hbm.at[:, :inner], query_weight, sems.at[3]))
    copies.append(pltpu.make_async_copy(latent_hbm, latent, sems.at[4]))
    for copy in copies[-1:] + copies[:-1]:
        copy.start()
    spread = group_matrix(channels, channels // GROUPS, True)
    scales[0] = exact_dot(stats[0], spread)
    inverse = 1.0 / jnp.sqrt(stats[1] * (1.0 / counted) + 1e-05)
    scales[1] = exact_dot(inverse, spread) * gain[...]
    place = lax.broadcasted_iota(jnp.int32, (columns, channels), 0)

    def put(value, row, i):
        rows = pl.ds(pl.multiple_of(row * slab + i * columns, columns), columns)
        before = jnp.where(place == 0, 0.0, pltpu.roll(value, 1, 0))
        after = jnp.where(place == columns - 1, 0.0, pltpu.roll(value, columns - 1, 0))
        ext[rows, 0:channels] = before.astype(jnp.bfloat16)
        ext[rows, channels : 2 * channels] = value.astype(jnp.bfloat16)
        ext[rows, 2 * channels : 3 * channels] = after.astype(jnp.bfloat16)

    def fill(i, carry):
        center = scales[0, pl.ds(i, 1), :]
        factor = scales[1, pl.ds(i, 1), :]
        put(top[i].astype(jnp.float32) * inside[0], 0, i)
        put(bottom[i].astype(jnp.float32) * inside[1], height + 1, i)
        for y in range(height):
            value = latent[i, y * columns : (y + 1) * columns, :].astype(jnp.float32)
            value = (value - center) * factor + shift[...]
            put(value / (1.0 + jnp.exp(-value)), y + 1, i)
        return carry

    copies[4].wait()
    lax.fori_loop(0, images, fill, 0)
    halves = 2
    part_rows = height // halves * slab

    def multiply(dy, m):
        first = dy * slab + m * part_rows
        return jnp.dot(
            ext[first : first + part_rows, :], weights[dy], preferred_element_type=jnp.float32
        )

    def finish(m):
        for y in range(m * height // halves, (m + 1) * height // halves):
            for i in range(images):
                tokens_of = slice(y * columns, (y + 1) * columns)
                rows = slice(y * slab + i * columns, y * slab + (i + 1) * columns)
                window = latent[i, tokens_of, :width].astype(jnp.float32) + acc[rows, :]
                window = (window + bias[i : i + 1, :]).astype(jnp.bfloat16)
                whole = jnp.concatenate([window, latent[i, tokens_of, width:]], axis=-1)
                hidden[i, tokens_of, :] = whole
                wide = whole.astype(jnp.float32)
                wide = wide - jnp.sum(wide, axis=-1, keepdims=True) * (1.0 / channels)
                variance = jnp.sum(wide * wide, axis=-1, keepdims=True) * (1.0 / channels)
                normal[i, tokens_of, :] = (wide * (1.0 / jnp.sqrt(variance + 1e-05))).astype(
                    jnp.bfloat16
                )

    for dy in range(3):
        copies[dy].wait()
        for m in range(halves):
            rows = slice(m * part_rows, (m + 1) * part_rows)
            if dy == 0:
                acc[rows, :] = multiply(dy, m)
            else:
                acc[rows, :] += multiply(dy, m)
            if dy == 2:
                finish(m)
    copies[3].wait()
    found = jnp.dot(
        normal[...].reshape(images * tokens, channels),
        query_weight[...],
        preferred_element_type=jnp.float32,
    )
    found = found.astype(jnp.bfloat16) * jnp.bfloat16((inner // HEADS) ** -0.5)
    queries[...] = found.reshape(images, tokens, inner)


def convolve(inside, stats, gain, shift, bias, latent, top, bottom, conv_weight, attn_in, counted):
    images, tokens, channels = latent.shape
    columns = top.shape[1]
    width = conv_weight.shape[-1]
    inner = attn_in.shape[1] // 3
    slab = images * columns
    vmem = pl.BlockSpec(memory_space=pltpu.VMEM)
    anywhere = pl.BlockSpec(memory_space=pl.ANY)

    def body(*refs):
        conv_kernel(counted, *refs)

    return pl.pallas_call(
        body,
        out_shape=(
            jax.ShapeDtypeStruct(latent.shape, jnp.bfloat16),
            jax.ShapeDtypeStruct(latent.shape, jnp.bfloat16),
            jax.ShapeDtypeStruct((images, tokens, inner), jnp.bfloat16),
        ),
        in_specs=[pl.BlockSpec(memory_space=pltpu.SMEM)] + [vmem] * 6 + [anywhere] * 3,
        out_specs=(vmem,) * 3,
        scratch_shapes=[
            pltpu.VMEM(latent.shape, jnp.bfloat16),
            pltpu.VMEM(((tokens // columns + 2) * slab, 3 * channels), jnp.bfloat16),
            pltpu.VMEM((3, 3 * channels, width), jnp.bfloat16),
            pltpu.VMEM((channels, inner), jnp.bfloat16),
            pltpu.VMEM((images * tokens, width), jnp.float32),
            pltpu.VMEM((2, 8, channels), jnp.float32),
            pltpu.SemaphoreType.DMA((5,)),
        ],
        compiler_params=pltpu.CompilerParams(vmem_limit_bytes=48 * MIB),
        cost_estimate=pl.CostEstimate(
            flops=2 * images * tokens * channels * (9 * width + inner),
            bytes_accessed=2 * (conv_weight.size + channels * inner + 5 * latent.size),
            transcendentals=latent.size,
        ),
        name="conv_queries",
    )(inside, stats, gain, shift, bias, top, bottom, latent, conv_weight, attn_in)


def project_kernel(normal, weight, out):
    images, tokens, channels = normal.shape
    found = jnp.dot(
        normal[...].reshape(images * tokens, channels),
        weight[...],
        preferred_element_type=jnp.float32,
    )
    out[0] = found.astype(jnp.bfloat16).reshape(out.shape[1:])


def project(normal, attn_in):
    images, tokens, channels = normal.shape
    inner = attn_in.shape[1] // 3
    return pl.pallas_call(
        project_kernel,
        grid=(2,),
        out_shape=jax.ShapeDtypeStruct((2, images, tokens, inner), jnp.bfloat16),
        in_specs=[
            pl.BlockSpec(normal.shape, lambda j: (0, 0, 0)),
            pl.BlockSpec((channels, inner), lambda j: (0, j + 1)),
        ],
        out_specs=pl.BlockSpec((1, images, tokens, inner), lambda j: (j, 0, 0, 0)),
        compiler_params=pltpu.CompilerParams(vmem_limit_bytes=24 * MIB),
        cost_estimate=pl.CostEstimate(
            flops=4 * images * tokens * channels * inner,
            bytes_accessed=4 * (channels * inner + normal.size),
            transcendentals=0,
        ),
        name="keys_values",
    )(normal, attn_in)


def attend_kernel(queries, first, second, third, far_keys, far_values, out, *logs):
    tokens, inner = queries.shape[1:]
    size = inner // HEADS
    pair = 2 * size
    lane = lax.broadcasted_iota(jnp.int32, (tokens, pair), 1)
    low = lane < size
    sources = (first, second, third)
    found = jnp.zeros((tokens, LANES), jnp.float32)
    spot = lax.broadcasted_iota(jnp.int32, (tokens, LANES), 1)
    for p in range(HEADS // 2):
        lanes = slice(p * pair, (p + 1) * pair)
        query = queries[0, :, lanes]
        blank = jnp.zeros_like(query)
        both = jnp.concatenate(
            [jnp.where(low, query, blank), jnp.where(low, blank, query)], axis=0
        )
        keys = jnp.concatenate(
            [s[0, 0, :, lanes] for s in sources] + [far_keys[0, :, lanes]], axis=0
        )
        values = jnp.concatenate(
            [s[1, 0, :, lanes] for s in sources] + [far_values[0, :, lanes]], axis=0
        )
        scores = lax.dot_general(
            both, keys, (((1,), (1,)), ((), ())), preferred_element_type=jnp.float32
        )
        peak = jnp.max(scores, axis=-1, keepdims=True)
        exponent = jnp.exp(scores - peak)
        total = jnp.sum(exponent, axis=-1, keepdims=True)
        context = jnp.dot(
            exponent.astype(jnp.bfloat16), values, preferred_element_type=jnp.float32
        )
        context = context * (1.0 / total)
        out[0, :tokens, lanes] = jnp.where(low, context[:tokens], context[tokens:]).astype(out.dtype)
        level = peak + jnp.log(total)
        found = jnp.where(spot == 2 * p, level[:tokens], found)
        found = jnp.where(spot == 2 * p + 1, level[tokens:], found)
    level = jnp.transpose(found)[:SLOTS, :]
    if logs:
        logs[0][0] = level
        return
    for part in range(3):
        term = level.astype(jnp.bfloat16)
        out[0, tokens:, part * LANES : (part + 1) * LANES] = term
        level = level - term.astype(jnp.float32)
    out[0, tokens:, 3 * LANES :] = jnp.zeros((SLOTS, inner - 3 * LANES), out.dtype)


def attend(queries, first, second, third, far_keys, far_values, start, images, packed):
    tokens, inner = queries.shape[1:]
    kv_spec = pl.BlockSpec((2, 1, tokens, inner), lambda i: (0, i + start, 0, 0))
    elements = images * HEADS * tokens * 4 * tokens
    if packed:
        out_shape = (jax.ShapeDtypeStruct((images, tokens + SLOTS, inner), jnp.bfloat16),)
    else:
        out_shape = (
            jax.ShapeDtypeStruct((images, tokens, inner), jnp.float32),
            jax.ShapeDtypeStruct((images, SLOTS, tokens), jnp.float32),
        )
    return pl.pallas_call(
        attend_kernel,
        grid=(images,),
        out_shape=out_shape,
        in_specs=[pl.BlockSpec((1, tokens, inner), lambda i: (i + start, 0, 0))]
        + [kv_spec] * 3
        + [pl.BlockSpec((1, tokens, inner), lambda i: (i, 0, 0))] * 2,
        out_specs=tuple(
            pl.BlockSpec((1,) + o.shape[1:], lambda i: (i, 0, 0)) for o in out_shape
        ),
        compiler_params=pltpu.CompilerParams(vmem_limit_bytes=24 * MIB),
        cost_estimate=pl.CostEstimate(
            flops=4 * elements * 256,
            bytes_accessed=images * tokens * inner * 24,
            transcendentals=elements,
        ),
        name="attend",
    )(queries, first, second, third, far_keys, far_values)


def join_kernel(
    own_first,
    logs_first,
    own_second,
    logs_second,
    far_first,
    far_second,
    hidden,
    weight,
    out,
    attended,
):
    images, tokens = hidden.shape[:2]
    half, tokens, inner = own_first.shape
    size = inner // HEADS
    pair = 2 * size
    low = lax.broadcasted_iota(jnp.int32, (tokens, pair), 1) < size
    for i in range(images):
        own, logs, far = (
            (own_first, logs_first, far_first)
            if i < half
            else (own_second, logs_second, far_second)
        )
        j = i % half
        here = logs[j]
        there = sum(
            far[j, tokens:, part * LANES : (part + 1) * LANES].astype(jnp.float32)
            for part in range(3)
        )
        top = jnp.maximum(here, there)
        here, there = jnp.exp(here - top), jnp.exp(there - top)
        share = there * (1.0 / (here + there))
        share = jnp.concatenate(
            [share, jnp.zeros((LANES - share.shape[0], tokens), jnp.float32)], axis=0
        )
        share = jnp.transpose(share)
        for p in range(HEADS // 2):
            lanes = slice(p * pair, (p + 1) * pair)
            part = jnp.where(
                low,
                jnp.broadcast_to(share[:, 2 * p : 2 * p + 1], (tokens, pair)),
                jnp.broadcast_to(share[:, 2 * p + 1 : 2 * p + 2], (tokens, pair)),
            )
            mine = own[j, :, lanes].astype(jnp.float32)
            theirs = far[j, :tokens, lanes].astype(jnp.float32)
            attended[i * tokens : (i + 1) * tokens, lanes] = (
                mine * (1.0 - part) + theirs * part
            ).astype(jnp.bfloat16)
    for i in range(images):
        rows = attended[i * tokens : (i + 1) * tokens, :]
        update = jnp.dot(rows, weight[...], preferred_element_type=jnp.float32)
        out[i] = (hidden[i].astype(jnp.float32) + update).astype(jnp.bfloat16)


def join(own, far, hidden, attn_out):
    images, tokens, channels = hidden.shape
    inner = attn_out.shape[0]
    return pl.pallas_call(
        join_kernel,
        out_shape=jax.ShapeDtypeStruct(hidden.shape, jnp.bfloat16),
        in_specs=[pl.BlockSpec(memory_space=pltpu.VMEM)] * 8,
        out_specs=pl.BlockSpec(memory_space=pltpu.VMEM),
        scratch_shapes=[pltpu.VMEM((images * tokens, inner), jnp.bfloat16)],
        compiler_params=pltpu.CompilerParams(vmem_limit_bytes=24 * MIB),
        cost_estimate=pl.CostEstimate(
            flops=2 * images * tokens * inner * channels,
            bytes_accessed=2 * attn_out.size + 4 * hidden.size + 6 * images * tokens * inner,
            transcendentals=0,
        ),
        name="join_project",
    )(*own[0], *own[1], far[0], far[1], hidden, attn_out)


def on_device(
    latent,
    stale_act,
    stale_kv,
    timestep,
    norm_gain,
    norm_shift,
    conv_weight,
    time_weight,
    attn_in,
    attn_out,
):
    images, height, columns, channels = latent.shape
    width = conv_weight.shape[3]
    inner = attn_out.shape[0]
    tokens = height * columns
    per_group = channels // GROUPS
    out_shape = latent.shape
    kv_shape = stale_kv.shape
    slot = lax.axis_index("band") % STACK
    latent = latent.reshape(images, tokens, channels)
    stale_kv = stale_kv.reshape(2, images, tokens, inner)

    stale_act = stale_act.reshape(images, tokens, channels)
    stats, last_rows, first_rows = local_stats(latent, stale_act, columns)
    top = rotated(last_rows, STACK)
    bottom = rotated(first_rows, -STACK)
    place = lax.axis_index("band") // STACK
    inside = jnp.stack([place > 0, place < IMG_ROWS // height - 1]).astype(jnp.float32)
    count = tokens * per_group
    for bit in (2, 4):
        stats = merged(stats, flipped(stats, bit), count)
        count *= 2
    stats, stale_kv = lax.optimization_barrier((stats, stale_kv))
    kv_up = rotated(stale_kv, 2 * STACK)
    kv_down = rotated(stale_kv, -2 * STACK)
    stats = merged(stats, flipped(stats, 1), count)
    count *= 2

    own_steps = lax.dynamic_index_in_dim(timestep, slot, 1, keepdims=False)
    bias = time_term(own_steps, time_weight)
    hidden, normal, queries = convolve(
        inside,
        stats,
        norm_gain.reshape(1, channels),
        norm_shift.reshape(1, channels),
        bias,
        latent,
        top,
        bottom,
        conv_weight.reshape(3, 3 * channels, width),
        attn_in,
        float(count),
    )
    half = images // 2
    far_queries = flipped(queries, 1)
    fresh_kv = project(normal, attn_in)
    kv_up, kv_down, fresh_kv = lax.optimization_barrier((kv_up, kv_down, fresh_kv))
    k_far = [rotated(kv_up[0, k * half : (k + 1) * half], 2 * STACK) for k in range(2)]
    v_far = [rotated(kv_down[1, k * half : (k + 1) * half], -2 * STACK) for k in range(2)]
    far = []
    for k in range(2):
        packed = attend(
            far_queries, stale_kv, kv_up, kv_down, k_far[k], v_far[k], k * half, half, True
        )[0]
        far.append(flipped(packed, 1))
    own = [
        attend(
            queries, fresh_kv, kv_up, kv_down, k_far[k], v_far[k], k * half, half, False
        )
        for k in range(2)
    ]
    block_out = join(own, far, hidden, attn_out)
    return (block_out.reshape(out_shape), fresh_kv.reshape(kv_shape))


def solution(mesh):
    return jax.shard_map(
        on_device,
        mesh=mesh,
        in_specs=(
            P("img", "band", None, None),
            P("img", "band", None, None),
            P(None, "img", "band", None, None),
            P("img", None),
            P(),
            P(),
            P(),
            P(),
            P(),
            P(),
        ),
        out_specs=(P("img", "band", None, None), P(None, "img", "band", None, None)),
        check_vma=False,
    )
```

```python
import math

import jax
import jax.numpy as jnp
from jax import lax
from jax.experimental import pallas as pl
from jax.experimental.pallas import tpu as pltpu
from jax.sharding import PartitionSpec as P

IMG_ROWS = 32
GROUPS = 32
HEADS = 10
TDIM = 1280
LANES = 128
SLOTS = 16
MIB = 1 << 20
STACK = 8


def rotated(value, by):
    count = lax.axis_size("band")
    return lax.ppermute(value, "band", [(i, (i + by) % count) for i in range(count)])


def flipped(value, bit):
    count = lax.axis_size("band")
    return lax.ppermute(value, "band", [(i, i ^ (bit * STACK)) for i in range(count)])


def outward(value):
    count = lax.axis_size("band")
    step = [-2 * STACK, 2 * STACK]
    pairs = [(i, (i + step[i // STACK % 2]) % count) for i in range(count)]
    return lax.ppermute(value, "band", pairs)


def time_term(timestep, time_weight):
    half_dim = TDIM // 2
    frequency = jnp.exp(-math.log(10000.0) * jnp.arange(half_dim, dtype=jnp.float32) / half_dim)
    angles = timestep.astype(jnp.float32)[:, None] * frequency[None, :]
    embedding = jnp.concatenate([jnp.cos(angles), jnp.sin(angles)], axis=1)
    return jnp.dot(
        jax.nn.silu(embedding), time_weight.astype(jnp.float32), precision=lax.Precision.HIGHEST
    )


def group_matrix(channels, per_group, transposed):
    shape = (LANES, channels) if transposed else (channels, LANES)
    channel = lax.broadcasted_iota(jnp.int32, shape, 1 if transposed else 0)
    first = lax.broadcasted_iota(jnp.int32, shape, 0 if transposed else 1) * per_group
    inside = (channel >= first) & (channel < first + per_group)
    return jnp.where(inside, 1.0, 0.0).astype(jnp.bfloat16)


def exact_dot(left, right):
    terms = []
    for _ in range(3):
        terms.append(left.astype(jnp.bfloat16).astype(jnp.float32))
        left = left - terms[-1]
    stacked = jnp.concatenate(terms, axis=0).astype(jnp.bfloat16)
    found = jnp.dot(stacked, right, preferred_element_type=jnp.float32)
    return found[0:8] + found[8:16] + found[16:24]


def stats_kernel(spot, latent_hbm, act_hbm, out, near, away, latent, rims, sums, sems):
    images, tokens, channels = latent.shape
    columns = near.shape[1]
    per_group = channels // GROUPS
    copies = [
        pltpu.make_async_copy(latent_hbm.at[i], latent.at[i], sems.at[i]) for i in range(images)
    ]
    for copy in copies:
        copy.start()
    start = spot[0] * (tokens - columns)
    sides = [
        pl.ds(pl.multiple_of(first, columns), columns)
        for first in (tokens - columns - start, start)
    ]
    cuts = [
        pltpu.make_async_copy(act_hbm.at[:, side, :], rims.at[k], sems.at[images + k])
        for k, side in enumerate(sides)
    ]
    for cut in cuts:
        cut.start()
    passed = [
        pltpu.make_async_copy(rims.at[k], rows, sems.at[images + 2 + k])
        for k, rows in enumerate((near, away))
    ]
    gather = group_matrix(channels, per_group, False)
    spread = group_matrix(channels, per_group, True)
    sums[...] = jnp.zeros_like(sums)
    for i in range(images):
        copies[i].wait()
        sums[i : i + 1, :] = jnp.sum(latent[i].astype(jnp.float32), axis=0, keepdims=True)
    for cut, onward in zip(cuts, passed):
        cut.wait()
        onward.start()
    mean = exact_dot(sums[...], gather) * (1.0 / (tokens * per_group))
    center = exact_dot(mean, spread)
    for i in range(images):
        deviation = latent[i].astype(jnp.float32) - center[i : i + 1, :]
        sums[i : i + 1, :] = jnp.sum(deviation * deviation, axis=0, keepdims=True)
    out[0] = mean
    out[1] = exact_dot(sums[...], gather)
    for onward in passed:
        onward.wait()


def local_stats(spot, latent, stale_act, columns):
    images, tokens, channels = latent.shape
    anywhere = pl.BlockSpec(memory_space=pltpu.HBM)
    vmem = pl.BlockSpec(memory_space=pltpu.VMEM)
    rim = jax.ShapeDtypeStruct((images, columns, channels), jnp.bfloat16)
    return pl.pallas_call(
        stats_kernel,
        out_shape=(jax.ShapeDtypeStruct((2, 8, LANES), jnp.float32), rim, rim),
        in_specs=[pl.BlockSpec(memory_space=pltpu.SMEM)] + [anywhere] * 2,
        out_specs=(vmem, anywhere, anywhere),
        scratch_shapes=[
            pltpu.VMEM(latent.shape, jnp.bfloat16),
            pltpu.VMEM((2,) + rim.shape, jnp.bfloat16),
            pltpu.VMEM((8, channels), jnp.float32),
            pltpu.SemaphoreType.DMA((images + 4,)),
        ],
        compiler_params=pltpu.CompilerParams(vmem_limit_bytes=60 * MIB),
        cost_estimate=pl.CostEstimate(
            flops=8 * latent.size, bytes_accessed=3 * latent.size, transcendentals=0
        ),
        name="group_stats",
    )(spot, latent, stale_act)


def merged(own, other, count):
    gap = own[0] - other[0]
    return jnp.stack([(own[0] + other[0]) * 0.5, own[1] + other[1] + gap * gap * (count * 0.5)])


def conv_kernel(
    counted,
    spot,
    stats,
    gain,
    shift,
    bias,
    near,
    away,
    latent_hbm,
    conv_hbm,
    attn_hbm,
    hidden,
    normal,
    queries,
    latent,
    ext,
    weights,
    query_weight,
    acc,
    scales,
    sems,
):
    images, tokens, channels = latent.shape
    columns = near.shape[1]
    height = tokens // columns
    width = acc.shape[1]
    slab = images * columns
    inner = query_weight.shape[1]
    copies = [
        pltpu.make_async_copy(conv_hbm.at[dy], weights.at[dy], sems.at[dy]) for dy in range(3)
    ]
    copies.append(pltpu.make_async_copy(attn_hbm.at[:, :inner], query_weight, sems.at[3]))
    copies.append(pltpu.make_async_copy(latent_hbm, latent, sems.at[4]))
    for copy in copies[-1:] + copies[:-1]:
        copy.start()
    spread = group_matrix(channels, channels // GROUPS, True)
    scales[0] = exact_dot(stats[0], spread)
    inverse = 1.0 / jnp.sqrt(stats[1] * (1.0 / counted) + 1e-05)
    scales[1] = exact_dot(inverse, spread) * gain[...]
    place = lax.broadcasted_iota(jnp.int32, (columns, channels), 0)

    def put(value, row, i):
        rows = pl.ds(pl.multiple_of(row * slab + i * columns, columns), columns)
        before = jnp.where(place == 0, 0.0, pltpu.roll(value, 1, 0))
        after = jnp.where(place == columns - 1, 0.0, pltpu.roll(value, columns - 1, 0))
        ext[rows, 0:channels] = before.astype(jnp.bfloat16)
        ext[rows, channels : 2 * channels] = value.astype(jnp.bfloat16)
        ext[rows, 2 * channels : 3 * channels] = after.astype(jnp.bfloat16)

    def fill(i, carry):
        center = scales[0, pl.ds(i, 1), :]
        factor = scales[1, pl.ds(i, 1), :]
        near_row = (1 - spot[0]) * (height + 1)
        put(near[i].astype(jnp.float32), near_row, i)
        inside = spot[1].astype(jnp.float32)
        put(away[i].astype(jnp.float32) * inside, height + 1 - near_row, i)
        for y in range(height):
            value = latent[i, y * columns : (y + 1) * columns, :].astype(jnp.float32)
            value = (value - center) * factor + shift[...]
            put(value / (1.0 + jnp.exp(-value)), y + 1, i)
        return carry

    copies[4].wait()
    lax.fori_loop(0, images, fill, 0)
    halves = 2
    part_rows = height // halves * slab

    def multiply(dy, m):
        first = dy * slab + m * part_rows
        return jnp.dot(
            ext[first : first + part_rows, :], weights[dy], preferred_element_type=jnp.float32
        )

    def finish(m):
        for y in range(m * height // halves, (m + 1) * height // halves):
            for i in range(images):
                tokens_of = slice(y * columns, (y + 1) * columns)
                rows = slice(y * slab + i * columns, y * slab + (i + 1) * columns)
                window = latent[i, tokens_of, :width].astype(jnp.float32) + acc[rows, :]
                window = (window + bias[i : i + 1, :]).astype(jnp.bfloat16)
                whole = jnp.concatenate([window, latent[i, tokens_of, width:]], axis=-1)
                hidden[i, tokens_of, :] = whole
                wide = whole.astype(jnp.float32)
                wide = wide - jnp.sum(wide, axis=-1, keepdims=True) * (1.0 / channels)
                variance = jnp.sum(wide * wide, axis=-1, keepdims=True) * (1.0 / channels)
                normal[i, tokens_of, :] = (wide * (1.0 / jnp.sqrt(variance + 1e-05))).astype(
                    jnp.bfloat16
                )

    for dy in range(3):
        copies[dy].wait()
        for m in range(halves):
            rows = slice(m * part_rows, (m + 1) * part_rows)
            if dy == 0:
                acc[rows, :] = multiply(dy, m)
            else:
                acc[rows, :] += multiply(dy, m)
            if dy == 2:
                finish(m)
    copies[3].wait()
    found = jnp.dot(
        normal[...].reshape(images * tokens, channels),
        query_weight[...],
        preferred_element_type=jnp.float32,
    )
    found = found.astype(jnp.bfloat16) * jnp.bfloat16((inner // HEADS) ** -0.5)
    queries[...] = found.reshape(images, tokens, inner)


def convolve(spot, stats, gain, shift, bias, latent, near, away, conv_weight, attn_in, counted):
    images, tokens, channels = latent.shape
    columns = near.shape[1]
    width = conv_weight.shape[-1]
    inner = attn_in.shape[1] // 3
    slab = images * columns
    vmem = pl.BlockSpec(memory_space=pltpu.VMEM)
    anywhere = pl.BlockSpec(memory_space=pl.ANY)

    def body(*refs):
        conv_kernel(counted, *refs)

    return pl.pallas_call(
        body,
        out_shape=(
            jax.ShapeDtypeStruct(latent.shape, jnp.bfloat16),
            jax.ShapeDtypeStruct(latent.shape, jnp.bfloat16),
            jax.ShapeDtypeStruct((images, tokens, inner), jnp.bfloat16),
        ),
        in_specs=[pl.BlockSpec(memory_space=pltpu.SMEM)] + [vmem] * 6 + [anywhere] * 3,
        out_specs=(vmem,) * 3,
        scratch_shapes=[
            pltpu.VMEM(latent.shape, jnp.bfloat16),
            pltpu.VMEM(((tokens // columns + 2) * slab, 3 * channels), jnp.bfloat16),
            pltpu.VMEM((3, 3 * channels, width), jnp.bfloat16),
            pltpu.VMEM((channels, inner), jnp.bfloat16),
            pltpu.VMEM((images * tokens, width), jnp.float32),
            pltpu.VMEM((2, 8, channels), jnp.float32),
            pltpu.SemaphoreType.DMA((5,)),
        ],
        compiler_params=pltpu.CompilerParams(vmem_limit_bytes=48 * MIB),
        cost_estimate=pl.CostEstimate(
            flops=2 * images * tokens * channels * (9 * width + inner),
            bytes_accessed=2 * (conv_weight.size + channels * inner + 5 * latent.size),
            transcendentals=latent.size,
        ),
        name="conv_queries",
    )(spot, stats, gain, shift, bias, near, away, latent, conv_weight, attn_in)


def project_kernel(normal, weight, out):
    images, tokens, channels = normal.shape
    found = jnp.dot(
        normal[...].reshape(images * tokens, channels),
        weight[...],
        preferred_element_type=jnp.float32,
    )
    out[0] = found.astype(jnp.bfloat16).reshape(out.shape[1:])


def project(normal, attn_in):
    images, tokens, channels = normal.shape
    inner = attn_in.shape[1] // 3
    return pl.pallas_call(
        project_kernel,
        grid=(2,),
        out_shape=jax.ShapeDtypeStruct((2, images, tokens, inner), jnp.bfloat16),
        in_specs=[
            pl.BlockSpec(normal.shape, lambda j: (0, 0, 0)),
            pl.BlockSpec((channels, inner), lambda j: (0, j + 1)),
        ],
        out_specs=pl.BlockSpec((1, images, tokens, inner), lambda j: (j, 0, 0, 0)),
        compiler_params=pltpu.CompilerParams(vmem_limit_bytes=24 * MIB),
        cost_estimate=pl.CostEstimate(
            flops=4 * images * tokens * channels * inner,
            bytes_accessed=4 * (channels * inner + normal.size),
            transcendentals=0,
        ),
        name="keys_values",
    )(normal, attn_in)


def attend_kernel(queries, first, second, third, far_keys, far_values, out, *logs):
    tokens, inner = queries.shape[1:]
    size = inner // HEADS
    pair = 2 * size
    lane = lax.broadcasted_iota(jnp.int32, (tokens, pair), 1)
    low = lane < size
    sources = (first, second, third)
    found = jnp.zeros((tokens, LANES), jnp.float32)
    spot = lax.broadcasted_iota(jnp.int32, (tokens, LANES), 1)
    for p in range(HEADS // 2):
        lanes = slice(p * pair, (p + 1) * pair)
        query = queries[0, :, lanes]
        blank = jnp.zeros_like(query)
        both = jnp.concatenate(
            [jnp.where(low, query, blank), jnp.where(low, blank, query)], axis=0
        )
        keys = jnp.concatenate(
            [s[0, 0, :, lanes] for s in sources] + [far_keys[0, :, lanes]], axis=0
        )
        values = jnp.concatenate(
            [s[1, 0, :, lanes] for s in sources] + [far_values[0, :, lanes]], axis=0
        )
        scores = lax.dot_general(
            both, keys, (((1,), (1,)), ((), ())), preferred_element_type=jnp.float32
        )
        peak = jnp.max(scores, axis=-1, keepdims=True)
        exponent = jnp.exp(scores - peak).astype(jnp.bfloat16)
        context = jnp.dot(
            exponent,
            jnp.concatenate([values, jnp.ones_like(values)], axis=1),
            preferred_element_type=jnp.float32,
        )
        total = context[:, pair:]
        context = context[:, :pair] * (1.0 / total)
        out[0, :tokens, lanes] = jnp.where(low, context[:tokens], context[tokens:]).astype(out.dtype)
        level = peak + jnp.log(total)
        found = jnp.where(spot == 2 * p, level[:tokens], found)
        found = jnp.where(spot == 2 * p + 1, level[tokens:], found)
    level = jnp.transpose(found)[:SLOTS, :]
    if logs:
        logs[0][0] = level
        return
    for part in range(3):
        term = level.astype(jnp.bfloat16)
        out[0, tokens:, part * LANES : (part + 1) * LANES] = term
        level = level - term.astype(jnp.float32)
    out[0, tokens:, 3 * LANES :] = jnp.zeros((SLOTS, inner - 3 * LANES), out.dtype)


def attend(queries, first, second, third, far_keys, far_values, start, images, packed):
    tokens, inner = queries.shape[1:]
    kv_spec = pl.BlockSpec((2, 1, tokens, inner), lambda i: (0, i + start, 0, 0))
    elements = images * HEADS * tokens * 4 * tokens
    if packed:
        out_shape = (jax.ShapeDtypeStruct((images, tokens + SLOTS, inner), jnp.bfloat16),)
    else:
        out_shape = (
            jax.ShapeDtypeStruct((images, tokens, inner), jnp.float32),
            jax.ShapeDtypeStruct((images, SLOTS, tokens), jnp.float32),
        )
    return pl.pallas_call(
        attend_kernel,
        grid=(images,),
        out_shape=out_shape,
        in_specs=[pl.BlockSpec((1, tokens, inner), lambda i: (i + start, 0, 0))]
        + [kv_spec] * 3
        + [pl.BlockSpec((1, tokens, inner), lambda i: (i, 0, 0))] * 2,
        out_specs=tuple(
            pl.BlockSpec((1,) + o.shape[1:], lambda i: (i, 0, 0)) for o in out_shape
        ),
        compiler_params=pltpu.CompilerParams(vmem_limit_bytes=24 * MIB),
        cost_estimate=pl.CostEstimate(
            flops=4 * elements * 256,
            bytes_accessed=images * tokens * inner * 24,
            transcendentals=elements,
        ),
        name="attend",
    )(queries, first, second, third, far_keys, far_values)


def join_kernel(own, logs, far, hidden, weight, *rest):
    out, attended = rest[-2:]
    images, tokens, inner = own.shape
    size = inner // HEADS
    pair = 2 * size
    low = lax.broadcasted_iota(jnp.int32, (tokens, pair), 1) < size
    for i in range(images):
        here = logs[i]
        there = sum(
            far[i, tokens:, part * LANES : (part + 1) * LANES].astype(jnp.float32)
            for part in range(3)
        )
        top = jnp.maximum(here, there)
        here, there = jnp.exp(here - top), jnp.exp(there - top)
        share = there * (1.0 / (here + there))
        share = jnp.concatenate(
            [share, jnp.zeros((LANES - share.shape[0], tokens), jnp.float32)], axis=0
        )
        share = jnp.transpose(share)
        for p in range(HEADS // 2):
            lanes = slice(p * pair, (p + 1) * pair)
            part = jnp.where(
                low,
                jnp.broadcast_to(share[:, 2 * p : 2 * p + 1], (tokens, pair)),
                jnp.broadcast_to(share[:, 2 * p + 1 : 2 * p + 2], (tokens, pair)),
            )
            mine = own[i, :, lanes].astype(jnp.float32)
            theirs = far[i, :tokens, lanes].astype(jnp.float32)
            attended[i * tokens : (i + 1) * tokens, lanes] = (
                mine * (1.0 - part) + theirs * part
            ).astype(jnp.bfloat16)
    update = jnp.dot(attended[...], weight[...], preferred_element_type=jnp.float32)
    out[...] = (hidden[...].astype(jnp.float32) + update.reshape(out.shape)).astype(jnp.bfloat16)


def join(own, logs, far, hidden, attn_out, block, earlier):
    images, tokens, inner = own.shape
    channels = hidden.shape[-1]
    part = pl.BlockSpec((images, tokens, channels), lambda i: (block, 0, 0))

    def whole(array):
        return pl.BlockSpec(array.shape, lambda i: (0,) * array.ndim)

    extra = [] if earlier is None else [earlier]
    return pl.pallas_call(
        join_kernel,
        grid=(1,),
        out_shape=jax.ShapeDtypeStruct(hidden.shape, jnp.bfloat16),
        in_specs=[whole(own), whole(logs), whole(far), part, whole(attn_out)]
        + [pl.BlockSpec(memory_space=pl.ANY) for _ in extra],
        out_specs=part,
        input_output_aliases={5: 0} if extra else {},
        scratch_shapes=[pltpu.VMEM((images * tokens, inner), jnp.bfloat16)],
        compiler_params=pltpu.CompilerParams(vmem_limit_bytes=24 * MIB),
        cost_estimate=pl.CostEstimate(
            flops=2 * images * tokens * inner * channels,
            bytes_accessed=2 * attn_out.size + 10 * images * tokens * inner,
            transcendentals=0,
        ),
        name="join_project",
    )(own, logs, far, hidden, attn_out, *extra)


def on_device(
    latent,
    stale_act,
    stale_kv,
    timestep,
    norm_gain,
    norm_shift,
    conv_weight,
    time_weight,
    attn_in,
    attn_out,
):
    images, height, columns, channels = latent.shape
    width = conv_weight.shape[3]
    inner = attn_out.shape[0]
    tokens = height * columns
    per_group = channels // GROUPS
    out_shape = latent.shape
    kv_shape = stale_kv.shape
    slot = lax.axis_index("band") % STACK
    latent = latent.reshape(images, tokens, channels)
    stale_kv = stale_kv.reshape(2, images, tokens, inner)

    stale_act = stale_act.reshape(images, tokens, channels)
    place = lax.axis_index("band") // STACK
    upper = place % 2
    inside = (place > 0) & (place < IMG_ROWS // height - 1)
    spot = jnp.stack([upper, inside.astype(jnp.int32)]).astype(jnp.int32)
    stats, near, away = local_stats(spot, latent, stale_act, columns)
    near = flipped(near, 1)
    away = flipped(outward(away), 1)
    count = tokens * per_group
    for bit in (2, 4):
        stats = merged(stats, flipped(stats, bit), count)
        count *= 2
    stats, stale_kv = lax.optimization_barrier((stats, stale_kv))
    kv_up = rotated(stale_kv, 2 * STACK)
    kv_down = rotated(stale_kv, -2 * STACK)
    stats, near, away = lax.optimization_barrier((stats, near, away))
    stats = merged(stats, flipped(stats, 1), count)
    count *= 2

    own_steps = lax.dynamic_index_in_dim(timestep, slot, 1, keepdims=False)
    bias = time_term(own_steps, time_weight)
    hidden, normal, queries = convolve(
        spot,
        stats,
        norm_gain.reshape(1, channels),
        norm_shift.reshape(1, channels),
        bias,
        latent,
        near,
        away,
        conv_weight.reshape(3, 3 * channels, width),
        attn_in,
        float(count),
    )
    half = images // 2
    far_queries = flipped(queries, 1)
    fresh_kv = project(normal, attn_in)
    kv_up, kv_down, fresh_kv = lax.optimization_barrier((kv_up, kv_down, fresh_kv))
    k_far = [rotated(kv_up[0, k * half : (k + 1) * half], 2 * STACK) for k in range(2)]
    v_far = [rotated(kv_down[1, k * half : (k + 1) * half], -2 * STACK) for k in range(2)]
    far = []
    for k in range(2):
        packed = attend(
            far_queries, stale_kv, kv_up, kv_down, k_far[k], v_far[k], k * half, half, True
        )[0]
        far.append(flipped(packed, 1))
    own = [
        attend(
            queries, fresh_kv, kv_up, kv_down, k_far[k], v_far[k], k * half, half, False
        )
        for k in range(2)
    ]
    block_out = None
    for k in range(2):
        block_out = join(*own[k], far[k], hidden, attn_out, k, block_out)
    return (block_out.reshape(out_shape), fresh_kv.reshape(kv_shape))


def solution(mesh):
    return jax.shard_map(
        on_device,
        mesh=mesh,
        in_specs=(
            P("img", "band", None, None),
            P("img", "band", None, None),
            P(None, "img", "band", None, None),
            P("img", None),
            P(),
            P(),
            P(),
            P(),
            P(),
            P(),
        ),
        out_specs=(P("img", "band", None, None), P(None, "img", "band", None, None)),
        check_vma=False,
    )
```

```python
import math

import jax
import jax.numpy as jnp
from jax import lax
from jax.experimental import pallas as pl
from jax.experimental.pallas import tpu as pltpu
from jax.sharding import PartitionSpec as P

IMG_ROWS = 32
GROUPS = 32
HEADS = 10
TDIM = 1280
LANES = 128
SLOTS = 16
MIB = 1 << 20
STACK = 8


def rotated(value, by):
    count = lax.axis_size("band")
    return lax.ppermute(value, "band", [(i, (i + by) % count) for i in range(count)])


def flipped(value, bit):
    count = lax.axis_size("band")
    return lax.ppermute(value, "band", [(i, i ^ (bit * STACK)) for i in range(count)])


def outward(value):
    count = lax.axis_size("band")
    step = [-2 * STACK, 2 * STACK]
    pairs = [(i, (i + step[i // STACK % 2]) % count) for i in range(count)]
    return lax.ppermute(value, "band", pairs)


def time_term(timestep, time_weight):
    half_dim = TDIM // 2
    frequency = jnp.exp(-math.log(10000.0) * jnp.arange(half_dim, dtype=jnp.float32) / half_dim)
    angles = timestep.astype(jnp.float32)[:, None] * frequency[None, :]
    embedding = jnp.concatenate([jnp.cos(angles), jnp.sin(angles)], axis=1)
    return jnp.dot(
        jax.nn.silu(embedding), time_weight.astype(jnp.float32), precision=lax.Precision.HIGHEST
    )


def group_matrix(channels, per_group, transposed):
    shape = (LANES, channels) if transposed else (channels, LANES)
    channel = lax.broadcasted_iota(jnp.int32, shape, 1 if transposed else 0)
    first = lax.broadcasted_iota(jnp.int32, shape, 0 if transposed else 1) * per_group
    inside = (channel >= first) & (channel < first + per_group)
    return jnp.where(inside, 1.0, 0.0).astype(jnp.bfloat16)


def exact_dot(left, right):
    terms = []
    for _ in range(3):
        terms.append(left.astype(jnp.bfloat16).astype(jnp.float32))
        left = left - terms[-1]
    stacked = jnp.concatenate(terms, axis=0).astype(jnp.bfloat16)
    found = jnp.dot(stacked, right, preferred_element_type=jnp.float32)
    return found[0:8] + found[8:16] + found[16:24]


def stats_kernel(latent_hbm, act_hbm, out, near, away, latent, rims, sums, sems):
    images, tokens, channels = latent.shape
    columns = near.shape[1]
    per_group = channels // GROUPS
    copies = [
        pltpu.make_async_copy(latent_hbm.at[i], latent.at[i], sems.at[i]) for i in range(images)
    ]
    for copy in copies:
        copy.start()
    start = lax.rem(lax.div(lax.axis_index("band"), STACK), 2) * (tokens - columns)
    sides = [
        pl.ds(pl.multiple_of(first, columns), columns)
        for first in (tokens - columns - start, start)
    ]
    cuts = [
        pltpu.make_async_copy(act_hbm.at[:, side, :], rims.at[k], sems.at[images + k])
        for k, side in enumerate(sides)
    ]
    for cut in cuts:
        cut.start()
    passed = [
        pltpu.make_async_copy(rims.at[k], rows, sems.at[images + 2 + k])
        for k, rows in enumerate((near, away))
    ]
    gather = group_matrix(channels, per_group, False)
    spread = group_matrix(channels, per_group, True)
    sums[...] = jnp.zeros_like(sums)
    for i in range(images):
        copies[i].wait()
        sums[i : i + 1, :] = jnp.sum(latent[i].astype(jnp.float32), axis=0, keepdims=True)
    for cut, onward in zip(cuts, passed):
        cut.wait()
        onward.start()
    mean = exact_dot(sums[...], gather) * (1.0 / (tokens * per_group))
    center = exact_dot(mean, spread)
    for i in range(images):
        deviation = latent[i].astype(jnp.float32) - center[i : i + 1, :]
        sums[i : i + 1, :] = jnp.sum(deviation * deviation, axis=0, keepdims=True)
    out[0] = mean
    out[1] = exact_dot(sums[...], gather)
    for onward in passed:
        onward.wait()


def local_stats(latent, stale_act, columns):
    images, tokens, channels = latent.shape
    anywhere = pl.BlockSpec(memory_space=pltpu.HBM)
    vmem = pl.BlockSpec(memory_space=pltpu.VMEM)
    rim = jax.ShapeDtypeStruct((images, columns, channels), jnp.bfloat16)
    return pl.pallas_call(
        stats_kernel,
        out_shape=(jax.ShapeDtypeStruct((2, 8, LANES), jnp.float32), rim, rim),
        in_specs=[anywhere] * 2,
        out_specs=(vmem, anywhere, anywhere),
        scratch_shapes=[
            pltpu.VMEM(latent.shape, jnp.bfloat16),
            pltpu.VMEM((2,) + rim.shape, jnp.bfloat16),
            pltpu.VMEM((8, channels), jnp.float32),
            pltpu.SemaphoreType.DMA((images + 4,)),
        ],
        compiler_params=pltpu.CompilerParams(vmem_limit_bytes=60 * MIB),
        cost_estimate=pl.CostEstimate(
            flops=8 * latent.size, bytes_accessed=3 * latent.size, transcendentals=0
        ),
        name="group_stats",
    )(latent, stale_act)


def merged(own, other, count):
    gap = own[0] - other[0]
    return jnp.stack([(own[0] + other[0]) * 0.5, own[1] + other[1] + gap * gap * (count * 0.5)])


def conv_kernel(
    counted,
    spot,
    stats,
    gain,
    shift,
    bias,
    near,
    away,
    latent_hbm,
    conv_hbm,
    attn_hbm,
    hidden,
    normal,
    queries,
    latent,
    ext,
    weights,
    query_weight,
    acc,
    scales,
    sems,
):
    images, tokens, channels = latent.shape
    columns = near.shape[1]
    height = tokens // columns
    width = acc.shape[1]
    slab = images * columns
    inner = query_weight.shape[1]
    copies = [
        pltpu.make_async_copy(conv_hbm.at[dy], weights.at[dy], sems.at[dy]) for dy in range(3)
    ]
    copies.append(pltpu.make_async_copy(attn_hbm.at[:, :inner], query_weight, sems.at[3]))
    copies.append(pltpu.make_async_copy(latent_hbm, latent, sems.at[4]))
    for copy in copies[-1:] + copies[:-1]:
        copy.start()
    spread = group_matrix(channels, channels // GROUPS, True)
    scales[0] = exact_dot(stats[0], spread)
    inverse = 1.0 / jnp.sqrt(stats[1] * (1.0 / counted) + 1e-05)
    scales[1] = exact_dot(inverse, spread) * gain[...]
    place = lax.broadcasted_iota(jnp.int32, (columns, channels), 0)

    def put(value, row, i):
        rows = pl.ds(pl.multiple_of(row * slab + i * columns, columns), columns)
        before = jnp.where(place == 0, 0.0, pltpu.roll(value, 1, 0))
        after = jnp.where(place == columns - 1, 0.0, pltpu.roll(value, columns - 1, 0))
        ext[rows, 0:channels] = before.astype(jnp.bfloat16)
        ext[rows, channels : 2 * channels] = value.astype(jnp.bfloat16)
        ext[rows, 2 * channels : 3 * channels] = after.astype(jnp.bfloat16)

    def fill(i, carry):
        center = scales[0, pl.ds(i, 1), :]
        factor = scales[1, pl.ds(i, 1), :]
        near_row = (1 - spot[0]) * (height + 1)
        put(near[i].astype(jnp.float32), near_row, i)
        inside = spot[1].astype(jnp.float32)
        put(away[i].astype(jnp.float32) * inside, height + 1 - near_row, i)
        for y in range(height):
            value = latent[i, y * columns : (y + 1) * columns, :].astype(jnp.float32)
            value = (value - center) * factor + shift[...]
            put(value / (1.0 + jnp.exp(-value)), y + 1, i)
        return carry

    copies[4].wait()
    lax.fori_loop(0, images, fill, 0)
    halves = 2
    part_rows = height // halves * slab

    def multiply(dy, m):
        first = dy * slab + m * part_rows
        return jnp.dot(
            ext[first : first + part_rows, :], weights[dy], preferred_element_type=jnp.float32
        )

    def finish(m):
        for y in range(m * height // halves, (m + 1) * height // halves):
            for i in range(images):
                tokens_of = slice(y * columns, (y + 1) * columns)
                rows = slice(y * slab + i * columns, y * slab + (i + 1) * columns)
                window = latent[i, tokens_of, :width].astype(jnp.float32) + acc[rows, :]
                window = (window + bias[i : i + 1, :]).astype(jnp.bfloat16)
                whole = jnp.concatenate([window, latent[i, tokens_of, width:]], axis=-1)
                hidden[i, tokens_of, :] = whole
                wide = whole.astype(jnp.float32)
                wide = wide - jnp.sum(wide, axis=-1, keepdims=True) * (1.0 / channels)
                variance = jnp.sum(wide * wide, axis=-1, keepdims=True) * (1.0 / channels)
                normal[i, tokens_of, :] = (wide * (1.0 / jnp.sqrt(variance + 1e-05))).astype(
                    jnp.bfloat16
                )

    for dy in range(3):
        copies[dy].wait()
        for m in range(halves):
            rows = slice(m * part_rows, (m + 1) * part_rows)
            if dy == 0:
                acc[rows, :] = multiply(dy, m)
            else:
                acc[rows, :] += multiply(dy, m)
            if dy == 2:
                finish(m)
    copies[3].wait()
    found = jnp.dot(
        normal[...].reshape(images * tokens, channels),
        query_weight[...],
        preferred_element_type=jnp.float32,
    )
    found = found.astype(jnp.bfloat16) * jnp.bfloat16((inner // HEADS) ** -0.5)
    queries[...] = found.reshape(images, tokens, inner)


def convolve(spot, stats, gain, shift, bias, latent, near, away, conv_weight, attn_in, counted):
    images, tokens, channels = latent.shape
    columns = near.shape[1]
    width = conv_weight.shape[-1]
    inner = attn_in.shape[1] // 3
    slab = images * columns
    vmem = pl.BlockSpec(memory_space=pltpu.VMEM)
    anywhere = pl.BlockSpec(memory_space=pl.ANY)

    def body(*refs):
        conv_kernel(counted, *refs)

    return pl.pallas_call(
        body,
        out_shape=(
            jax.ShapeDtypeStruct(latent.shape, jnp.bfloat16),
            jax.ShapeDtypeStruct(latent.shape, jnp.bfloat16),
            jax.ShapeDtypeStruct((images, tokens, inner), jnp.bfloat16),
        ),
        in_specs=[pl.BlockSpec(memory_space=pltpu.SMEM)] + [vmem] * 6 + [anywhere] * 3,
        out_specs=(vmem,) * 3,
        scratch_shapes=[
            pltpu.VMEM(latent.shape, jnp.bfloat16),
            pltpu.VMEM(((tokens // columns + 2) * slab, 3 * channels), jnp.bfloat16),
            pltpu.VMEM((3, 3 * channels, width), jnp.bfloat16),
            pltpu.VMEM((channels, inner), jnp.bfloat16),
            pltpu.VMEM((images * tokens, width), jnp.float32),
            pltpu.VMEM((2, 8, channels), jnp.float32),
            pltpu.SemaphoreType.DMA((5,)),
        ],
        compiler_params=pltpu.CompilerParams(vmem_limit_bytes=48 * MIB),
        cost_estimate=pl.CostEstimate(
            flops=2 * images * tokens * channels * (9 * width + inner),
            bytes_accessed=2 * (conv_weight.size + channels * inner + 5 * latent.size),
            transcendentals=latent.size,
        ),
        name="conv_queries",
    )(spot, stats, gain, shift, bias, near, away, latent, conv_weight, attn_in)


def project_kernel(normal, weight, out):
    images, tokens, channels = normal.shape
    found = jnp.dot(
        normal[...].reshape(images * tokens, channels),
        weight[...],
        preferred_element_type=jnp.float32,
    )
    out[0] = found.astype(jnp.bfloat16).reshape(out.shape[1:])


def project(normal, attn_in):
    images, tokens, channels = normal.shape
    inner = attn_in.shape[1] // 3
    return pl.pallas_call(
        project_kernel,
        grid=(2,),
        out_shape=jax.ShapeDtypeStruct((2, images, tokens, inner), jnp.bfloat16),
        in_specs=[
            pl.BlockSpec(normal.shape, lambda j: (0, 0, 0)),
            pl.BlockSpec((channels, inner), lambda j: (0, j + 1)),
        ],
        out_specs=pl.BlockSpec((1, images, tokens, inner), lambda j: (j, 0, 0, 0)),
        compiler_params=pltpu.CompilerParams(vmem_limit_bytes=24 * MIB),
        cost_estimate=pl.CostEstimate(
            flops=4 * images * tokens * channels * inner,
            bytes_accessed=4 * (channels * inner + normal.size),
            transcendentals=0,
        ),
        name="keys_values",
    )(normal, attn_in)


def attend_kernel(queries, first, second, third, far_keys, far_values, out, *logs):
    tokens, inner = queries.shape[1:]
    size = inner // HEADS
    pair = 2 * size
    lane = lax.broadcasted_iota(jnp.int32, (tokens, pair), 1)
    low = lane < size
    sources = (first, second, third)
    found = jnp.zeros((tokens, LANES), jnp.float32)
    spot = lax.broadcasted_iota(jnp.int32, (tokens, LANES), 1)
    for p in range(HEADS // 2):
        lanes = slice(p * pair, (p + 1) * pair)
        query = queries[0, :, lanes]
        blank = jnp.zeros_like(query)
        both = jnp.concatenate(
            [jnp.where(low, query, blank), jnp.where(low, blank, query)], axis=0
        )
        keys = jnp.concatenate(
            [s[0, 0, :, lanes] for s in sources] + [far_keys[0, :, lanes]], axis=0
        )
        values = jnp.concatenate(
            [s[1, 0, :, lanes] for s in sources] + [far_values[0, :, lanes]], axis=0
        )
        scores = lax.dot_general(
            both, keys, (((1,), (1,)), ((), ())), preferred_element_type=jnp.float32
        )
        peak = jnp.max(scores, axis=-1, keepdims=True)
        exponent = jnp.exp(scores - peak).astype(jnp.bfloat16)
        context = jnp.dot(
            exponent,
            jnp.concatenate([values, jnp.ones_like(values)], axis=1),
            preferred_element_type=jnp.float32,
        )
        total = context[:, pair:]
        context = context[:, :pair] * (1.0 / total)
        out[0, :tokens, lanes] = jnp.where(low, context[:tokens], context[tokens:]).astype(out.dtype)
        level = peak + jnp.log(total)
        found = jnp.where(spot == 2 * p, level[:tokens], found)
        found = jnp.where(spot == 2 * p + 1, level[tokens:], found)
    level = jnp.transpose(found)[:SLOTS, :]
    if logs:
        logs[0][0] = level
        return
    for part in range(3):
        term = level.astype(jnp.bfloat16)
        out[0, tokens:, part * LANES : (part + 1) * LANES] = term
        level = level - term.astype(jnp.float32)
    out[0, tokens:, 3 * LANES :] = jnp.zeros((SLOTS, inner - 3 * LANES), out.dtype)


def attend(queries, first, second, third, far_keys, far_values, start, images, packed):
    tokens, inner = queries.shape[1:]
    kv_spec = pl.BlockSpec((2, 1, tokens, inner), lambda i: (0, i + start, 0, 0))
    elements = images * HEADS * tokens * 4 * tokens
    if packed:
        out_shape = (jax.ShapeDtypeStruct((images, tokens + SLOTS, inner), jnp.bfloat16),)
    else:
        out_shape = (
            jax.ShapeDtypeStruct((images, tokens, inner), jnp.float32),
            jax.ShapeDtypeStruct((images, SLOTS, tokens), jnp.float32),
        )
    return pl.pallas_call(
        attend_kernel,
        grid=(images,),
        out_shape=out_shape,
        in_specs=[pl.BlockSpec((1, tokens, inner), lambda i: (i + start, 0, 0))]
        + [kv_spec] * 3
        + [pl.BlockSpec((1, tokens, inner), lambda i: (i, 0, 0))] * 2,
        out_specs=tuple(
            pl.BlockSpec((1,) + o.shape[1:], lambda i: (i, 0, 0)) for o in out_shape
        ),
        compiler_params=pltpu.CompilerParams(vmem_limit_bytes=24 * MIB),
        cost_estimate=pl.CostEstimate(
            flops=4 * elements * 256,
            bytes_accessed=images * tokens * inner * 24,
            transcendentals=elements,
        ),
        name="attend",
    )(queries, first, second, third, far_keys, far_values)


def join_kernel(own, logs, far, hidden, weight, *rest):
    out, attended = rest[-2:]
    images, tokens, inner = own.shape
    size = inner // HEADS
    pair = 2 * size
    low = lax.broadcasted_iota(jnp.int32, (tokens, pair), 1) < size
    for i in range(images):
        here = logs[i]
        there = sum(
            far[i, tokens:, part * LANES : (part + 1) * LANES].astype(jnp.float32)
            for part in range(3)
        )
        top = jnp.maximum(here, there)
        here, there = jnp.exp(here - top), jnp.exp(there - top)
        share = there * (1.0 / (here + there))
        share = jnp.concatenate(
            [share, jnp.zeros((LANES - share.shape[0], tokens), jnp.float32)], axis=0
        )
        share = jnp.transpose(share)
        for p in range(HEADS // 2):
            lanes = slice(p * pair, (p + 1) * pair)
            part = jnp.where(
                low,
                jnp.broadcast_to(share[:, 2 * p : 2 * p + 1], (tokens, pair)),
                jnp.broadcast_to(share[:, 2 * p + 1 : 2 * p + 2], (tokens, pair)),
            )
            mine = own[i, :, lanes].astype(jnp.float32)
            theirs = far[i, :tokens, lanes].astype(jnp.float32)
            attended[i * tokens : (i + 1) * tokens, lanes] = (
                mine * (1.0 - part) + theirs * part
            ).astype(jnp.bfloat16)
    update = jnp.dot(attended[...], weight[...], preferred_element_type=jnp.float32)
    out[...] = (hidden[...].astype(jnp.float32) + update.reshape(out.shape)).astype(jnp.bfloat16)


def join(own, logs, far, hidden, attn_out, block, earlier):
    images, tokens, inner = own.shape
    channels = hidden.shape[-1]
    part = pl.BlockSpec((images, tokens, channels), lambda i: (block, 0, 0))

    def whole(array):
        return pl.BlockSpec(array.shape, lambda i: (0,) * array.ndim)

    extra = [] if earlier is None else [earlier]
    return pl.pallas_call(
        join_kernel,
        grid=(1,),
        out_shape=jax.ShapeDtypeStruct(hidden.shape, jnp.bfloat16),
        in_specs=[whole(own), whole(logs), whole(far), part, whole(attn_out)]
        + [pl.BlockSpec(memory_space=pl.ANY) for _ in extra],
        out_specs=part,
        input_output_aliases={5: 0} if extra else {},
        scratch_shapes=[pltpu.VMEM((images * tokens, inner), jnp.bfloat16)],
        compiler_params=pltpu.CompilerParams(vmem_limit_bytes=24 * MIB),
        cost_estimate=pl.CostEstimate(
            flops=2 * images * tokens * inner * channels,
            bytes_accessed=2 * attn_out.size + 10 * images * tokens * inner,
            transcendentals=0,
        ),
        name="join_project",
    )(own, logs, far, hidden, attn_out, *extra)


def on_device(
    latent,
    stale_act,
    stale_kv,
    timestep,
    norm_gain,
    norm_shift,
    conv_weight,
    time_weight,
    attn_in,
    attn_out,
):
    images, height, columns, channels = latent.shape
    width = conv_weight.shape[3]
    inner = attn_out.shape[0]
    tokens = height * columns
    per_group = channels // GROUPS
    out_shape = latent.shape
    kv_shape = stale_kv.shape
    slot = lax.axis_index("band") % STACK
    latent = latent.reshape(images, tokens, channels)
    stale_kv = stale_kv.reshape(2, images, tokens, inner)

    stale_act = stale_act.reshape(images, tokens, channels)
    place = lax.axis_index("band") // STACK
    upper = place % 2
    inside = (place > 0) & (place < IMG_ROWS // height - 1)
    spot = jnp.stack([upper, inside.astype(jnp.int32)]).astype(jnp.int32)
    stats, near, away = local_stats(latent, stale_act, columns)
    near = flipped(near, 1)
    away = flipped(outward(away), 1)
    count = tokens * per_group
    for bit in (2, 4):
        stats = merged(stats, flipped(stats, bit), count)
        count *= 2
    stats, stale_kv = lax.optimization_barrier((stats, stale_kv))
    kv_up = rotated(stale_kv, 2 * STACK)
    kv_down = rotated(stale_kv, -2 * STACK)
    stats, near, away = lax.optimization_barrier((stats, near, away))
    stats = merged(stats, flipped(stats, 1), count)
    count *= 2

    own_steps = lax.dynamic_index_in_dim(timestep, slot, 1, keepdims=False)
    bias = time_term(own_steps, time_weight)
    hidden, normal, queries = convolve(
        spot,
        stats,
        norm_gain.reshape(1, channels),
        norm_shift.reshape(1, channels),
        bias,
        latent,
        near,
        away,
        conv_weight.reshape(3, 3 * channels, width),
        attn_in,
        float(count),
    )
    half = images // 2
    far_queries = flipped(queries, 1)
    fresh_kv = project(normal, attn_in)
    kv_up, kv_down, fresh_kv = lax.optimization_barrier((kv_up, kv_down, fresh_kv))
    k_far = [rotated(kv_up[0, k * half : (k + 1) * half], 2 * STACK) for k in range(2)]
    v_far = [rotated(kv_down[1, k * half : (k + 1) * half], -2 * STACK) for k in range(2)]
    far = []
    for k in range(2):
        packed = attend(
            far_queries, stale_kv, kv_up, kv_down, k_far[k], v_far[k], k * half, half, True
        )[0]
        far.append(flipped(packed, 1))
    own = [
        attend(
            queries, fresh_kv, kv_up, kv_down, k_far[k], v_far[k], k * half, half, False
        )
        for k in range(2)
    ]
    block_out = None
    for k in range(2):
        block_out = join(*own[k], far[k], hidden, attn_out, k, block_out)
    return (block_out.reshape(out_shape), fresh_kv.reshape(kv_shape))


def solution(mesh):
    return jax.shard_map(
        on_device,
        mesh=mesh,
        in_specs=(
            P("img", "band", None, None),
            P("img", "band", None, None),
            P(None, "img", "band", None, None),
            P("img", None),
            P(),
            P(),
            P(),
            P(),
            P(),
            P(),
        ),
        out_specs=(P("img", "band", None, None), P(None, "img", "band", None, None)),
        check_vma=False,
    )
```
